128 devices in a mesh: img: 8 (over y, x_lo), ori: 16 (over z, x_hi, core).
Axes of the slice: x: 4 (x_hi: 2, x_lo: 2; x = x_hi * 2 + x_lo), y: 4, z: 4, core: 2. Of those that a mesh axis runs over, the one named last changes fastest.
Arguments:
- images: bfloat16 [3072, 16384], P('img'), may hold values from -16 to 16
- noise_precision: float32 [3072], P('img'), as said below
- prior_weight: float32 [128], replicated, may hold values from 0.25 to 4
- bead_coords: float32 [128, 3, 3000], replicated, may hold values from -96 to 96
- euler_angles: float32 [3, 64], P(None, 'ori'), may hold values from -3.140625 to 3.140625
- template_conf: int32 [6144], P('ori'), may hold values from 0 to 127, as said below
- template_orient: int32 [6144], P('ori'), may hold values from 0 to 3
Outputs:
- new_weights: float32 [128], replicated
- log_evidence: float32 [3072], P('img')
The draws below stay inside these ranges and needn't reach their ends.
Inputs may be any that keep to these rules, and one draw needn't show every extreme that they name: `template_conf`: every conformation is rendered in one template or more. `noise_precision`: each value lies between 80 / 128 and 160 / 128.
All inputs are finite; a program needn't handle non-finite values.
Results may differ from the reference program's by a relative error of at most 0.0025.
The reference program's roundings to bfloat16 on the way count: a program that leaves them out, or rounds other values in their place, can miss the bound.
Values may be sent and summed in bfloat16 or wider, within the bound.
A program may use at most 128 MiB of HBM per device.

```python
import math
import jax
import jax.numpy as jnp
from jax import lax

GRID = 128
BEADS = 3000
K = 128
ORI_DEV = 4
TPL_DEV = 48
IMG_DEV = 384
PIX = 16384
ORIS = 64
TEMPLATES = 6144
IMAGES = 3072
N_IMG = 8


def draw_noise_precision(key, part):
    first_key = jax.random.fold_in(key, 0)
    values = jnp.exp(jax.random.uniform(first_key, (IMAGES,), jnp.float32, math.log(80.0 / GRID), math.log(160.0 / GRID)))
    return values


def draw_template_conf(key, part):
    first_key, second_key, third_key = jax.random.split(jax.random.fold_in(key, 7), 3)
    every = jax.random.permutation(first_key, K).astype(jnp.int32)
    others = jax.random.randint(second_key, (TEMPLATES - K,), 0, K, dtype=jnp.int32)
    joined = jnp.concatenate([every, others])
    order = jax.random.permutation(third_key, TEMPLATES)
    return joined[order].astype(jnp.int32)


def touch_ends(entries, rng, low, high):
    place = [jax.random.randint(jax.random.fold_in(rng, axis), (), 0, length) for axis, length in enumerate(entries.shape)]
    main_axis = entries.shape.index(max(entries.shape))
    next_to = place[:main_axis] + [(place[main_axis] + 1) % entries.shape[main_axis]] + place[main_axis + 1:]
    return entries.at[tuple(place)].set(low).at[tuple(next_to)].set(high)


def block_scale(rng, dims, shards, smallest, top_value):
    def one(axis_at, blocks):
        heights = jax.random.uniform(jax.random.fold_in(jax.random.fold_in(rng, 6), axis_at), (blocks,), jnp.float32, smallest / len(shards), top_value / len(shards))
        return jnp.repeat(jnp.exp(heights), dims[axis_at] // blocks).reshape((-1,) + (1,) * (len(dims) - axis_at - 1))

    gain = one(*shards[0])
    for cut in shards[1:]:
        gain = gain * one(*cut)
    return gain


def normal_values(key, dims, scale, most, pieces=(), kind=jnp.bfloat16):
    entries = jax.random.normal(key, dims, jnp.float32) * scale
    if len(pieces) > 0:
        entries = block_scale(key, dims, pieces, -0.22, 0.18) * entries
    return jnp.clip(entries, min=-most, max=most).astype(kind)


def setup_inputs(seed: int = 0) -> dict:
    arg_keys = jax.random.split(jax.random.key(seed), 8)
    images = normal_values(arg_keys[0], (IMAGES, PIX), 3.0, 16.0, ((0, 8),))
    noise_precision = draw_noise_precision(jax.random.fold_in(arg_keys[7], 71), 0)
    prior_weight = jnp.clip(jnp.exp(jax.random.uniform(arg_keys[2], (K,), jnp.float32, math.log(0.25), math.log(4.0))), 0.25, 4.0)
    bead_coords = normal_values(arg_keys[3], (K, 3, BEADS), (GRID / 8), 96.0, (), jnp.float32)
    euler_angles = jnp.clip(jax.random.uniform(arg_keys[4], (3, ORIS), jnp.float32, -3.140625, 3.140625), -3.140625, 3.140625)
    template_conf = draw_template_conf(jax.random.fold_in(arg_keys[7], 71), 0)
    template_orient = touch_ends(jax.random.randint(arg_keys[6], (TEMPLATES,), 0, ORI_DEV), jax.random.fold_in(arg_keys[6], 1), 0, ORI_DEV - 1).astype(jnp.int32)
    return {"images": images, "noise_precision": noise_precision, "prior_weight": prior_weight, "bead_coords": bead_coords, "euler_angles": euler_angles, "template_conf": template_conf, "template_orient": template_orient}


BLOB_SIGMA = 1.5

def rotation_rows(angles):
    ca, sa = (jnp.cos(angles[0]), jnp.sin(angles[0]))
    cb, sb = (jnp.cos(angles[1]), jnp.sin(angles[1]))
    cg, sg = (jnp.cos(angles[2]), jnp.sin(angles[2]))
    first = (ca * cb * cg - sa * sg, -ca * cb * sg - sa * cg, ca * sb)
    second = (sa * cb * cg + ca * sg, -sa * cb * sg + ca * cg, sa * sb)
    return (first, second)

def render(chosen, angles):
    first, second = rotation_rows(angles)
    centre = (GRID - 1) / 2.0
    coord_u = first[0][:, None] * chosen[:, 0] + first[1][:, None] * chosen[:, 1] + first[2][:, None] * chosen[:, 2] + centre
    coord_v = second[0][:, None] * chosen[:, 0] + second[1][:, None] * chosen[:, 1] + second[2][:, None] * chosen[:, 2] + centre
    pixels = jnp.arange(GRID, dtype=jnp.float32)
    factor = 0.5 / (BLOB_SIGMA * BLOB_SIGMA)
    gauss_u = jnp.exp(-jnp.square(coord_u[:, :, None] - pixels) * factor).astype(jnp.bfloat16)
    gauss_v = jnp.exp(-jnp.square(coord_v[:, :, None] - pixels) * factor).astype(jnp.bfloat16)
    raw = jnp.einsum('nbp,nbq->npq', gauss_u.astype(jnp.float32), gauss_v.astype(jnp.float32), precision=lax.Precision.HIGHEST)
    raw = raw.reshape(raw.shape[0], GRID * GRID)
    centred = raw - lax.optimization_barrier(jnp.mean(raw, axis=1, keepdims=True))
    spread = lax.optimization_barrier(jnp.mean(centred * centred, axis=1, keepdims=True))
    return (centred * lax.rsqrt(spread + 1e-05)).astype(jnp.bfloat16)

def reference(images, noise_precision, prior_weight, bead_coords, euler_angles, template_conf, template_orient):
    count = template_conf.shape[0]
    column = jnp.arange(count, dtype=jnp.int32) // (TPL_DEV * N_IMG)
    orient = (column * ORI_DEV + template_orient).astype(jnp.int32)
    angles = euler_angles[:, orient]
    groups = count // TPL_DEV
    conf_groups = template_conf.reshape(groups, TPL_DEV)
    angle_groups = angles.reshape(3, groups, TPL_DEV).transpose(1, 0, 2)
    templates = lax.map(lambda item: render(bead_coords[item[0]], item[1]), (conf_groups, angle_groups))
    templates = templates.reshape(count, GRID * GRID)
    log_prior = jnp.log(prior_weight) - jnp.log(jnp.sum(prior_weight))
    bias = log_prior[template_conf]
    blocks = images.reshape(N_IMG, IMG_DEV, GRID * GRID)
    prec_blocks = noise_precision.reshape(N_IMG, IMG_DEV)

    def score(item):
        block, prec = item
        raw = lax.dot_general(block, templates, (((1,), (1,)), ((), ())), preferred_element_type=jnp.float32)
        logits = prec[:, None] * raw + bias[None, :]
        row_top = lax.optimization_barrier(jnp.max(logits, axis=1))
        evidence = row_top + jnp.log(lax.optimization_barrier(jnp.sum(jnp.exp(logits - row_top[:, None]), axis=1)))
        column_mass = lax.optimization_barrier(jnp.sum(jnp.exp(logits - evidence[:, None]), axis=0))
        return (evidence, column_mass)
    evidence, masses = lax.map(score, (blocks, prec_blocks))
    mass = lax.optimization_barrier(jnp.sum(masses, axis=0))
    totals = jax.ops.segment_sum(mass, template_conf, num_segments=K)
    new_weights = K * totals / (IMG_DEV * N_IMG)
    return (new_weights, evidence.reshape(IMG_DEV * N_IMG))
```

```python
import functools
import math

import jax
import jax.numpy as jnp
from jax import lax
from jax.experimental import pallas as pl
from jax.experimental.pallas import tpu as pltpu
from jax.sharding import PartitionSpec as P

GRID = 128
PIX = GRID * GRID
K = 128
BEADS = 3000
BPAD = 3072
TPL_DEV = 48
N_IMG = 8
N_ORI = 16
IMG_DEV = 384
GROUP = 16
NGROUP = TPL_DEV // GROUP
BLOB_SIGMA = 1.5
SCALE = -0.5 / (BLOB_SIGMA * BLOB_SIGMA) * math.log2(math.e)
MESH = pl.DeviceIdType.MESH
TRANS = (((1,), (1,)), ((), ()))
HIGH = lax.Precision.HIGHEST
CHUNK = 512
SCORE_CHUNK = 2048

LB = 72 * 128
LBH = 36 * 128
LC = PIX - LB
LCH = LC // 2
FULL_B = (0, LB)
B0 = (0, LBH)
B1 = (LBH, LB - LBH)
FULL_C = (LB, LC)
C0 = (LB, LCH)
C1 = (LB + LCH, LC - LCH)

N_KIND = 18


def rotation_rows(angles):
    ca, sa = (jnp.cos(angles[0]), jnp.sin(angles[0]))
    cb, sb = (jnp.cos(angles[1]), jnp.sin(angles[1]))
    cg, sg = (jnp.cos(angles[2]), jnp.sin(angles[2]))
    first = (ca * cb * cg - sa * sg, -ca * cb * sg - sa * cg, ca * sb)
    second = (sa * cb * cg + ca * sg, -sa * cb * sg + ca * cg, sa * sb)
    return jnp.stack(first + second)


def gauss(row, pix):
    d = row - pix
    return jnp.exp2((d * d) * SCALE).astype(jnp.bfloat16)


def kernel(
    images, prec, prior, beads, coef, conf, orient,
    out_w, out_e,
    img_s, tpl, beads_s, u_s, v_s, raw, lt, confb, orib, stat, mass_a, mass_b,
    in_sem, send_sem, recv_sem, ssend, srecv, asend, arecv, bsend, brecv,
):
    r = lax.axis_index("img")
    o = lax.axis_index("ori")
    part = r + 1 - 2 * (r % 2)
    up = (r + 2) % N_IMG
    down = (r + 6) % N_IMG
    up_part = (part + 2) % N_IMG
    down_part = (part + 6) % N_IMG
    far = (r + 4) % N_IMG

    barrier = pltpu.get_barrier_semaphore()
    for j in range(1, N_IMG):
        pl.semaphore_signal(barrier, inc=1, device_id=((r + j) % N_IMG, o), device_id_type=MESH)
    for j in range(1, N_ORI):
        pl.semaphore_signal(barrier, inc=1, device_id=(r, (o + j) % N_ORI), device_id_type=MESH)

    bead_copies = [
        pltpu.make_async_copy(beads.at[c], beads_s.at[c, pl.ds(0, BEADS)], in_sem.at[c]) for c in range(3)
    ]
    for copy in bead_copies:
        copy.start()
    image_copy = pltpu.make_async_copy(images, img_s, in_sem.at[3])
    image_copy.start()

    confb[...] = jnp.broadcast_to(conf[...].astype(jnp.float32), (GRID, TPL_DEV * N_IMG)).T
    orib[...] = jnp.broadcast_to(orient[...].astype(jnp.float32), (GRID, TPL_DEV * N_IMG)).T
    mine = pl.ds(pl.multiple_of(r * TPL_DEV, GROUP), TPL_DEV)
    lane = lax.broadcasted_iota(jnp.int32, (TPL_DEV, K), 1).astype(jnp.float32)
    onehot = (confb[mine, :] == lane).astype(jnp.float32)
    own_orient = orib[mine, :]
    coefs = []
    for c in range(6):
        value = jnp.full((TPL_DEV, K), coef[c, 3], jnp.float32)
        for q in (2, 1, 0):
            value = jnp.where(own_orient == float(q), coef[c, q], value)
        coefs.append(jnp.concatenate([value] * (CHUNK // K), axis=1))
    for c in range(3):
        beads_s[c, BEADS:BPAD, :] = jnp.zeros((BPAD - BEADS, K), jnp.float32)
    for copy in bead_copies:
        copy.wait()
    centre = (GRID - 1) / 2.0

    def place(c, carry):
        rows = pl.ds(pl.multiple_of(c * CHUNK, CHUNK), CHUNK)
        x, y, z = [
            lax.dot_general(onehot, beads_s[a, rows, :], TRANS, precision=HIGH, preferred_element_type=jnp.float32)
            for a in range(3)
        ]
        index = c * CHUNK + lax.broadcasted_iota(jnp.int32, (TPL_DEV, CHUNK), 1)
        u = coefs[0] * x + coefs[1] * y + coefs[2] * z + centre
        v = coefs[3] * x + coefs[4] * y + coefs[5] * z + centre
        u_s[:, rows] = jnp.where(index < BEADS, u, 1e4)
        v_s[:, rows] = jnp.where(index < BEADS, v, 1e4)
        return carry

    lax.fori_loop(0, BPAD // CHUNK, place, 0)

    pix = lax.broadcasted_iota(jnp.int32, (GRID, CHUNK), 0).astype(jnp.float32)

    def render(g):
        def pair(j, carry):
            for k in range(2):
                t = j * 2 + k
                acc = None
                for c in range(BPAD // CHUNK):
                    cols = pl.ds(c * CHUNK, CHUNK)
                    gu = gauss(u_s[pl.ds(g * GROUP + t, 1), cols], pix)
                    gv = gauss(v_s[pl.ds(g * GROUP + t, 1), cols], pix)
                    part_sum = lax.dot_general(gu, gv, TRANS, preferred_element_type=jnp.float32)
                    acc = part_sum if acc is None else acc + part_sum
                raw[pl.ds(pl.multiple_of(t * GRID, GRID), GRID), :] = acc
            return carry

        lax.fori_loop(0, GROUP // 2, pair, 0)
        unroll = 8

        def add(p, acc):
            for k in range(unroll):
                acc = acc + raw[pl.ds(p * unroll + k, GROUP, stride=GRID), :]
            return acc

        zero = jnp.zeros((GROUP, GRID), jnp.float32)
        total = lax.fori_loop(0, GRID // unroll, add, zero)
        mean = jnp.broadcast_to(jnp.sum(total, axis=1, keepdims=True) * (1.0 / PIX), (GROUP, GRID))

        def square(p, acc):
            for k in range(unroll):
                x = raw[pl.ds(p * unroll + k, GROUP, stride=GRID), :] - mean
                acc = acc + x * x
            return acc

        spread = lax.fori_loop(0, GRID // unroll, square, zero)
        var = jnp.sum(spread, axis=1, keepdims=True) * (1.0 / PIX)
        scale = jnp.broadcast_to(lax.rsqrt(var + 1e-05), (GROUP, GRID))
        rows = pl.ds(pl.multiple_of(r * GROUP, GROUP), GROUP)

        def put(p, carry):
            for k in range(unroll):
                x = (raw[pl.ds(p * unroll + k, GROUP, stride=GRID), :] - mean) * scale
                cols = pl.ds(pl.multiple_of((p * unroll + k) * GRID, GRID), GRID)
                tpl[g, rows, cols] = x.astype(jnp.bfloat16)
            return carry

        lax.fori_loop(0, GRID // unroll, put, 0)

    routes = [
        (r, FULL_B, part),
        (r, FULL_B, up),
        (r, FULL_B, down),
        (r, FULL_C, up),
        (r, FULL_C, down),
        (r, FULL_C, part),
        (part, FULL_B, up),
        (part, FULL_B, down),
        (down, B0, up),
        (up, B1, down),
        (down, C0, up),
        (down, FULL_C, part),
        (up, C1, down),
        (up, FULL_C, part),
        (down_part, B0, up),
        (up_part, B1, down),
        (far, C0, part),
        (far, C1, part),
    ]

    def copy_of(g, k):
        source, (start, size), target = routes[k]
        piece = tpl.at[g, pl.ds(pl.multiple_of(source * GROUP, GROUP), GROUP), pl.ds(start, size)]
        return pltpu.make_async_remote_copy(
            src_ref=piece,
            dst_ref=piece,
            send_sem=send_sem.at[g, k],
            recv_sem=recv_sem.at[g, k],
            device_id=(target, o),
            device_id_type=MESH,
        )

    def send(g, *kinds):
        for k in kinds:
            copy_of(g, k).start()

    def arrive(g, *kinds):
        for k in kinds:
            copy_of(g, k).wait_recv()

    def own(g):
        send(g, 0, 1, 2, 3, 4, 5)

    def level1(g):
        arrive(g, 0, 1, 2)
        send(g, 6, 7, 8, 9)
        arrive(g, 3, 4)
        send(g, 10, 12, 11, 13)

    def level2(g):
        arrive(g, 6, 7)
        send(g, 14, 15)
        arrive(g, 10, 12)
        send(g, 16, 17)

    def last(g):
        arrive(g, 5, 8, 9, 11, 13, 14, 15, 16, 17)

    prior_row = prior[...]
    log_prior = jnp.log(prior_row) - jnp.log(jnp.sum(prior_row, axis=1, keepdims=True))
    lane_k = lax.broadcasted_iota(jnp.int32, (N_IMG * GROUP, K), 1).astype(jnp.float32)

    def is_conf(g):
        pieces = [confb[n * TPL_DEV + g * GROUP : n * TPL_DEV + (g + 1) * GROUP, :] for n in range(N_IMG)]
        return jnp.concatenate(pieces, axis=0) == lane_k

    def score(g):
        def body(c, acc):
            cols = pl.ds(pl.multiple_of(c * SCORE_CHUNK, SCORE_CHUNK), SCORE_CHUNK)
            return acc + lax.dot_general(
                tpl[g, :, cols], img_s[:, cols], TRANS, preferred_element_type=jnp.float32
            )

        acc = lax.fori_loop(
            0, PIX // SCORE_CHUNK, body, jnp.zeros((N_IMG * GROUP, IMG_DEV), jnp.float32)
        )
        bias = jnp.sum(jnp.where(is_conf(g), log_prior, 0.0), axis=1, keepdims=True)
        lt[g] = acc * prec[...] + bias

    render(0)
    pl.semaphore_wait(barrier, N_IMG + N_ORI - 2)
    own(0)
    render(1)
    level1(0)
    own(1)
    render(2)
    level2(0)
    level1(1)
    own(2)
    image_copy.wait()
    last(0)
    score(0)
    level2(1)
    level1(2)
    last(1)
    score(1)
    level2(2)
    last(2)
    score(2)

    logits = lt[...].reshape(NGROUP * N_IMG * GROUP, IMG_DEV)
    top = jnp.max(logits, axis=0, keepdims=True)
    stat[o, :, :IMG_DEV] = top
    stat[o, :, IMG_DEV:] = jnp.sum(jnp.exp(logits - top), axis=0, keepdims=True)

    def exchange(buf, me, n, send_sems, recv_sems, device):
        copies = [
            pltpu.make_async_remote_copy(
                src_ref=buf.at[me],
                dst_ref=buf.at[me],
                send_sem=send_sems.at[j],
                recv_sem=recv_sems.at[j],
                device_id=device((me + j) % n),
                device_id_type=MESH,
            )
            for j in range(1, n)
        ]
        for copy in copies:
            copy.start()
        for copy in copies:
            copy.wait_recv()
        return copies

    pending = exchange(stat, o, N_ORI, ssend, srecv, lambda d: (r, d))
    tops = [stat[n, :, :IMG_DEV] for n in range(N_ORI)]
    peak = functools.reduce(jnp.maximum, tops)
    total = functools.reduce(
        jnp.add, [stat[n, :, IMG_DEV:] * jnp.exp(tops[n] - peak) for n in range(N_ORI)]
    )
    evidence = peak + jnp.log(total)
    out_e[...] = evidence

    partial = jnp.zeros((1, K), jnp.float32)
    for g in range(NGROUP):
        mass = jnp.sum(jnp.exp(lt[g] - evidence), axis=1, keepdims=True)
        partial = partial + jnp.sum(jnp.where(is_conf(g), mass, 0.0), axis=0, keepdims=True)
    mass_a[r] = partial
    pending += exchange(mass_a, r, N_IMG, asend, arecv, lambda d: (d, o))
    mass_b[o] = functools.reduce(jnp.add, [mass_a[n] for n in range(N_IMG)])
    pending += exchange(mass_b, o, N_ORI, bsend, brecv, lambda d: (r, d))
    totals = functools.reduce(jnp.add, [mass_b[n] for n in range(N_ORI)])
    out_w[...] = K * totals / (IMG_DEV * N_IMG)

    for copy in pending:
        copy.wait_send()
    for g in range(NGROUP):
        for k in range(N_KIND):
            copy_of(g, k).wait_send()


def local(
    images, noise_precision, prior_weight, bead_coords, euler_angles, template_conf, template_orient
):
    vmem = pl.BlockSpec(memory_space=pltpu.VMEM)
    anywhere = pl.BlockSpec(memory_space=pl.ANY)
    f32 = jnp.float32
    dma = pltpu.SemaphoreType.DMA
    weights, evidence = pl.pallas_call(
        kernel,
        out_shape=(jax.ShapeDtypeStruct((1, K), f32), jax.ShapeDtypeStruct((1, IMG_DEV), f32)),
        in_specs=[anywhere, vmem, vmem, anywhere, pl.BlockSpec(memory_space=pltpu.SMEM), vmem, vmem],
        out_specs=(vmem, vmem),
        scratch_shapes=[
            pltpu.VMEM((IMG_DEV, PIX), jnp.bfloat16),
            pltpu.VMEM((NGROUP, N_IMG * GROUP, PIX), jnp.bfloat16),
            pltpu.VMEM((3, BPAD, K), f32),
            pltpu.VMEM((TPL_DEV, BPAD), f32),
            pltpu.VMEM((TPL_DEV, BPAD), f32),
            pltpu.VMEM((GROUP * GRID, GRID), f32),
            pltpu.VMEM((NGROUP, N_IMG * GROUP, IMG_DEV), f32),
            pltpu.VMEM((N_IMG * TPL_DEV, K), f32),
            pltpu.VMEM((N_IMG * TPL_DEV, K), f32),
            pltpu.VMEM((N_ORI, 1, 2 * IMG_DEV), f32),
            pltpu.VMEM((N_IMG, 1, K), f32),
            pltpu.VMEM((N_ORI, 1, K), f32),
            dma((4,)),
            dma((NGROUP, N_KIND)),
            dma((NGROUP, N_KIND)),
            dma((N_ORI,)),
            dma((N_ORI,)),
            dma((N_IMG,)),
            dma((N_IMG,)),
            dma((N_ORI,)),
            dma((N_ORI,)),
        ],
        compiler_params=pltpu.CompilerParams(
            collective_id=0, has_side_effects=True, vmem_limit_bytes=62 << 20
        ),
    )(
        images,
        noise_precision.reshape(1, IMG_DEV),
        prior_weight.reshape(1, K),
        jnp.transpose(bead_coords, (1, 2, 0)),
        rotation_rows(euler_angles),
        template_conf.reshape(1, -1),
        template_orient.reshape(1, -1),
    )
    return (weights.reshape(K), evidence.reshape(IMG_DEV))


def solution(mesh):
    placed = (P("img", None), P("img"), P(), P(), P(None, "ori"), P("ori"), P("ori"))
    return jax.shard_map(
        local, mesh=mesh, in_specs=placed, out_specs=(P(), P("img")), check_vma=False
    )
```
